32 devices in a mesh: col: 8 (over y, x, core), row: 4 (over z).
Axes of the slice: x: 2, y: 2, z: 4, core: 2. Of those that a mesh axis runs over, the one named last changes fastest.
Arguments:
- matrix: float32 [16, 512, 4096], P(None, 'row', 'col'), may hold values from -0.4 to 2.4, as said below
- pivots: int32 [8, 512], replicated, may hold values from 0 to 511, as said below
- seeds: float32 [8, 512, 512], P('col'), may hold values from -1 to 2, as said below
Outputs:
- factors: float32 [16, 512, 4096], P(None, 'row', 'col')
The draws below stay inside these ranges and needn't reach their ends.
Inputs may be any that keep to these rules, and one draw needn't show every extreme that they name: Each row of pivots is an ordering of 0 .. 511. Block (r, j) of matrix is zero where r and j differ by more than 8. seeds[k] approximates the inverse of block (k, k) of matrix after the replacement of rows by pivots[k].
All inputs are finite; a program needn't handle non-finite values.
Results may differ from the reference program's by a relative error of at most 0.0001.
Values sent between devices are 32-bit elements; how exact they have to be, the bound alone decides.
A program may use at most 64 MiB of HBM per device.

```python
import math
import jax
import jax.numpy as jnp
from jax import lax

B = 512
HB = 8
SWEEPS = 2
PANELS = 8
NBLK = 16
COLS = 4096


def build_all(key):
    key_perm, key_vals, key_diag, key_noise = jax.random.split(jax.random.fold_in(key, 4242), 4)
    pivots = jax.vmap(lambda one_key: jax.random.permutation(one_key, B))(jax.random.split(key_perm, PANELS)).astype(jnp.int32)
    values = jnp.clip(jax.random.normal(key_vals, (NBLK, B, COLS), jnp.float32), -4.0, 4.0)
    block_rows = jnp.arange(NBLK)[:, None, None]
    block_cols = (jnp.arange(COLS) // B)[None, None, :]
    offset = block_rows - block_cols
    spread = jnp.where(offset == 0, 0.35, 0.165) / math.sqrt(B)
    spread = jnp.where(jnp.abs(offset) <= HB, spread, 0.0)
    diag_values = jnp.exp(jax.random.uniform(key_diag, (NBLK, B), jnp.float32, 0.0, math.log(2.0)))
    on_diagonal = (jnp.arange(B)[None, :, None] == (jnp.arange(COLS) % B)[None, None, :]) & (offset == 0)
    permuted = values * spread + jnp.where(on_diagonal, diag_values[:, :, None], 0.0)
    leading = permuted[:PANELS].reshape(PANELS, B, PANELS, B)
    diag_blocks = leading[jnp.arange(PANELS), :, jnp.arange(PANELS), :]
    identity = jnp.eye(B, dtype=jnp.float32)
    approx = identity[None] / diag_values[:PANELS, None, :]
    for sweep_index in range(12):
        product = jnp.einsum('pij,pjk->pik', diag_blocks, approx, precision=lax.Precision.HIGHEST)
        approx = jnp.einsum('pij,pjk->pik', approx, 2.0 * identity[None] - product, precision=lax.Precision.HIGHEST)
    noise = jnp.clip(jax.random.normal(key_noise, (PANELS, B, B), jnp.float32), -4.0, 4.0) * (0.25 / math.sqrt(B))
    seeds = approx - jnp.einsum('pij,pjk->pik', approx, noise, precision=lax.Precision.HIGHEST)
    inverse_order = jnp.argsort(pivots, axis=1).astype(jnp.int32)
    top_rows = jnp.take_along_axis(permuted[:PANELS], inverse_order[:, :, None], axis=1)
    matrix = jnp.concatenate([top_rows, permuted[PANELS:]], axis=0)
    return (matrix, pivots, seeds)


def draw_matrix(key, part):
    return build_all(key)[0]


def draw_pivots(key, part):
    return build_all(key)[1]


def draw_seeds(key, part):
    return build_all(key)[2]


def setup_inputs(seed: int = 0) -> dict:
    key_list = jax.random.split(jax.random.key(seed), 4)
    return {
        "matrix": draw_matrix(jax.random.fold_in(key_list[3], 71), 0),
        "pivots": draw_pivots(jax.random.fold_in(key_list[3], 71), 0),
        "seeds": draw_seeds(jax.random.fold_in(key_list[3], 71), 0),
    }


def dot_high(left, right):
    return jnp.dot(left, right, precision=lax.Precision.HIGHEST, preferred_element_type=jnp.float32)


def reference(matrix, pivots, seeds):
    factors = matrix
    identity = jnp.eye(B, dtype=jnp.float32)
    column_ids = jnp.arange(COLS)
    for panel_index in range(PANELS):
        panel_cols = slice(panel_index * B, (panel_index + 1) * B)
        row_block = factors[panel_index]
        swapped = jnp.take(row_block, pivots[panel_index], axis=0)
        col_mask = (column_ids >= panel_index * B)[None, :]
        row_block = jnp.where(col_mask, swapped, row_block)
        factors = factors.at[panel_index].set(row_block)
        pivot_block = row_block[:, panel_cols]
        approx = seeds[panel_index]
        for sweep_index in range(SWEEPS):
            approx = dot_high(approx, 2.0 * identity - dot_high(pivot_block, approx))
        below_rows = factors[panel_index + 1:panel_index + HB + 1, :, panel_cols].reshape(HB * B, B)
        multipliers = dot_high(below_rows, approx)
        factors = factors.at[panel_index + 1:panel_index + HB + 1, :, panel_cols].set(multipliers.reshape(HB, B, B))
        last_panel = min(panel_index + HB, PANELS - 1)
        if last_panel >= panel_index + 1:
            trail_cols = slice((panel_index + 1) * B, (last_panel + 1) * B)
            upper_rows = row_block[:, trail_cols]
            change = dot_high(multipliers, upper_rows).reshape(HB, B, -1)
            factors = factors.at[panel_index + 1:panel_index + HB + 1, :, trail_cols].add(-change)
    return factors
```

```python
import functools

import jax
import jax.numpy as jnp
from jax import lax
from jax.experimental import pallas as pl
from jax.experimental.pallas import tpu as pltpu
from jax.sharding import PartitionSpec as P

HB = 8
F32 = jnp.float32
BF16 = jnp.bfloat16
MESH = pl.DeviceIdType.MESH


def split(x):
    high = x.astype(BF16)
    return high, (x - high.astype(F32)).astype(BF16)


def dot(left, right):
    return jnp.dot(left, right, preferred_element_type=F32)


def dot3(left, right):
    return dot(left[0], right[0]) + (dot(left[0], right[1]) + dot(left[1], right[0]))


def split3(x):
    high = x.astype(BF16)
    rest = x - high.astype(F32)
    middle = rest.astype(BF16)
    return high, middle, (rest - middle.astype(F32)).astype(BF16)


def kernel(
    ncol, nrow, a_hbm, piv_ref, seed_ref, out_ref,
    upper, mult, u_high, u_low, approx, x_high, x_low, e_high, e_low, f_high, f_low,
    usend, urecv, msend, mrecv, lsem,
):
    square = ncol == 8 and nrow == 4 and HB >= ncol - 1
    col = lax.axis_index("col")
    row = lax.axis_index("row")
    share, width = out_ref.shape[1], out_ref.shape[2]
    first = jnp.maximum(col - HB, 0)
    chip, core = col // 2, lax.rem(col, 2)

    load = pltpu.make_async_copy(a_hbm, out_ref, lsem)
    load.start()
    barrier = pltpu.get_barrier_semaphore()
    for step in range(1, nrow):
        pl.semaphore_signal(
            barrier, inc=1, device_id=(col, lax.rem(row + step, nrow)), device_id_type=MESH
        )
    for step in range(1, ncol):
        pl.semaphore_signal(
            barrier, inc=1, device_id=(lax.rem(col + step, ncol), row), device_id_type=MESH
        )
    pl.semaphore_wait(barrier, nrow + ncol - 2)
    load.wait()

    def share_copy(k, slot, source, target):
        return pltpu.make_async_remote_copy(
            src_ref=upper.at[k, source],
            dst_ref=upper.at[k, source],
            send_sem=usend.at[k, slot],
            recv_sem=urecv.at[k, source],
            device_id=(col, target),
            device_id_type=MESH,
        )

    def own_sends(k, act):
        if not square:
            for step in range(1, nrow):
                act(share_copy(k, step, row, lax.rem(row + step, nrow)))
            return
        end = (row == 0) | (row == 3)
        ahead = jnp.where(row < 2, 1, -1)

        @pl.when(end)
        def _():
            for step in (3, 2, 1):
                act(share_copy(k, step, row, row + ahead * step))

        @pl.when(~end)
        def _():
            act(share_copy(k, 1, row, row + ahead))
            act(share_copy(k, 2, row, row - ahead))

    def relayed(k):
        ahead = jnp.where(row < 2, 1, -1)
        return share_copy(k, 3, row + ahead, row - ahead)

    def start_gather(k):
        upper[k, row] = out_ref[k]
        own_sends(k, lambda copy: copy.start())

    def wait_share(k, source):
        share_copy(k, 0, source, source).wait_recv()

    def relay(k):
        if square:
            @pl.when((row == 1) | (row == 2))
            def _():
                wait_share(k, jnp.where(row < 2, row + 1, row - 1))
                relayed(k).start()

    def sources():
        if not square:
            return [(None, lax.rem(row + step, nrow)) for step in range(1, nrow)]
        end = (row == 0) | (row == 3)
        ahead = jnp.where(row < 2, 1, -1)
        return [
            (None, jnp.where(end, row + 3 * ahead, row - ahead)),
            (None, jnp.where(end, row + ahead, row + 2 * ahead)),
            (end, row + 2 * ahead),
        ]

    def finish_gather(k):
        for when, source in sources():
            if when is None:
                wait_share(k, source)
            else:
                pl.when(when)(lambda source=source: wait_share(k, source))

    def mult_copy(k, c, slot, target):
        return pltpu.make_async_remote_copy(
            src_ref=mult.at[k, c],
            dst_ref=mult.at[k, c],
            send_sem=msend.at[k, c, slot],
            recv_sem=mrecv.at[k, c],
            device_id=(target, row),
            device_id_type=MESH,
        )

    def forward(k, c, act):
        if not square:
            @pl.when((col + 1 < ncol) & (col + 1 <= k + HB))
            def _():
                act(mult_copy(k, c, 0, col + 1))

            return
        owner = k // 2
        mine = k == col
        odd = lax.rem(c, 2) == 1
        late = odd & (c > 1)
        leads = ~mine & (core == 0)
        near = owner == 0
        along_y = (mine & (chip < 2)) | (leads & near & (chip == 1) & ~odd)
        along_x = (mine & ((chip == 0) | (chip == 2))) | (
            leads & ((near & odd & (chip == 2)) | ((owner == 1) & late & (chip == 3)))
        )
        across = mine & (chip == 1) & ~late

        @pl.when(core == 0)
        def _():
            act(mult_copy(k, c, 0, col + 1))

        @pl.when(along_x | across)
        def _():
            other = jnp.where(across, 2, chip + 1 - 2 * lax.rem(chip, 2))
            act(mult_copy(k, c, 1, 2 * other))

        @pl.when(along_y)
        def _():
            act(mult_copy(k, c, 2, 2 * (chip + 2)))

    def start(copy):
        copy.start()

    def one_hot(k):
        ordering = jnp.broadcast_to(piv_ref[pl.ds(k, 1), :], (width, width))
        hits = lax.broadcasted_iota(jnp.int32, (width, width), 0) == ordering
        return jnp.where(hits, 1.0, 0.0).astype(BF16)

    def store_swapped(k):
        ordering = piv_ref[pl.ds(k, 1), :]
        mine = ordering[:, :share]
        for other in range(1, nrow):
            mine = jnp.where(row == other, ordering[:, other * share:(other + 1) * share], mine)
        hits = lax.broadcasted_iota(jnp.int32, (width, share), 0) == jnp.broadcast_to(mine, (width, share))
        hits = jnp.where(hits, 1.0, 0.0).astype(BF16)
        parts = split3(upper[k].reshape(width, width))
        contract = (((0,), (0,)), ((), ()))
        pick = lambda part: lax.dot_general(hits, part, contract, preferred_element_type=F32)
        out_ref[k] = pick(parts[0]) + (pick(parts[1]) + pick(parts[2]))

    def split_upper(k):
        high, low = split(upper[k].reshape(width, width))
        u_high[k] = high
        u_low[k] = low

    def chunk(k, c):
        mult_copy(k, c, 0, col).wait_recv()
        forward(k, c, start)
        change = dot3(split(mult[k, c]), (u_high[k], u_low[k]))
        out_ref[k + 1 + c] = out_ref[k + 1 + c] - change

    start_gather(first)

    scatter = one_hot(col)
    seed_parts = split3(seed_ref[0])
    contract = (((1,), (1,)), ((), ()))
    total = lax.dot_general(seed_parts[2], scatter, contract, preferred_element_type=F32)
    total += lax.dot_general(seed_parts[1], scatter, contract, preferred_element_type=F32)
    total += lax.dot_general(seed_parts[0], scatter, contract, preferred_element_type=F32)
    approx[...] = total
    high, low = split(total)
    x_high[...] = high
    x_low[...] = low
    relay(first)

    def update(k, carry):
        finish_gather(k)
        split_upper(k)

        @pl.when(k > first)
        def _():
            chunk(k - 1, 1)

        chunk(k, 0)
        start_gather(k + 1)

        @pl.when(k > first)
        def _():
            @pl.loop(2, HB)
            def _(c):
                chunk(k - 1, c)

        store_swapped(k)
        relay(k + 1)
        return carry

    lax.fori_loop(first, col, update, 0)

    @pl.when(col > first)
    def _():
        chunk(col - 1, 1)

    seed = (x_high[...], x_low[...])
    ahead = dot3(split(out_ref[col + 1]), seed)

    def residual(source):
        high, low = split(upper[col, source])
        rows = lax.broadcasted_iota(jnp.int32, (share, width), 0) + source * share
        unit = jnp.where(rows == lax.broadcasted_iota(jnp.int32, (share, width), 1), 1.0, 0.0)
        left = unit - dot3((high, low), (x_high[...], x_low[...]))
        high, low = split(left)
        e_high[source] = high
        e_low[source] = low

    residual(row)
    if square:
        @pl.when((row == 1) | (row == 2))
        def _():
            residual(jnp.where(row < 2, row + 1, row - 1))
    for when, source in sources():
        def arrive(source=source):
            wait_share(col, source)
            residual(source)

        if when is None:
            arrive()
        else:
            pl.when(when)(arrive)

    error = (e_high[...].reshape(width, width), e_low[...].reshape(width, width))
    high, low = split(dot3(error, error))
    f_high[...] = high
    f_low[...] = low
    ahead = ahead + dot3(split(ahead), error)
    mult[col, 0] = ahead + dot3(split(ahead), (high, low))
    forward(col, 0, start)

    better = approx[...]
    better = better + dot3((x_high[...], x_low[...]), (e_high[...].reshape(width, width), e_low[...].reshape(width, width)))
    better = better + dot3(split(better), (f_high[...], f_low[...]))
    high, low = split(better)
    x_high[...] = high
    x_low[...] = low

    @pl.loop(1, HB)
    def _(c):
        @pl.when((col > first) & (c + 1 < HB))
        def _():
            chunk(col - 1, c + 1)

        mult[col, c] = dot3(split(out_ref[col + 1 + c]), (x_high[...], x_low[...]))
        forward(col, c, start)

    store_swapped(col)
    f_high[...] = one_hot(col)

    @pl.loop(0, HB)
    def _(c):
        parts = split3(mult[col, c])
        target = f_high[...]
        out_ref[col + 1 + c] = dot(parts[0], target) + (dot(parts[1], target) + dot(parts[2], target))

    def drain(k, carry):
        own_sends(k, lambda copy: copy.wait_send())
        if square:
            @pl.when((row == 1) | (row == 2))
            def _():
                relayed(k).wait_send()

        @pl.loop(0, HB)
        def _(c):
            forward(k, c, lambda copy: copy.wait_send())

        return carry

    lax.fori_loop(first, col + 1, drain, 0)


def local(matrix, pivots, seeds):
    ncol = lax.axis_size("col")
    nrow = lax.axis_size("row")
    nblk, share, width = matrix.shape
    vmem = pl.BlockSpec(memory_space=pltpu.VMEM)
    half = pltpu.VMEM((width, width), BF16)
    return pl.pallas_call(
        functools.partial(kernel, ncol, nrow),
        out_shape=jax.ShapeDtypeStruct(matrix.shape, F32),
        in_specs=[pl.BlockSpec(memory_space=pl.ANY), vmem, vmem],
        out_specs=vmem,
        scratch_shapes=[
            pltpu.VMEM((ncol, nrow, share, width), F32),
            pltpu.VMEM((ncol, HB, share, width), F32),
            pltpu.VMEM((ncol, width, width), BF16),
            pltpu.VMEM((ncol, width, width), BF16),
            pltpu.VMEM((width, width), F32),
            half,
            half,
            pltpu.VMEM((nrow, share, width), BF16),
            pltpu.VMEM((nrow, share, width), BF16),
            half,
            half,
            pltpu.SemaphoreType.DMA((ncol, nrow)),
            pltpu.SemaphoreType.DMA((ncol, nrow)),
            pltpu.SemaphoreType.DMA((ncol, HB, 3)),
            pltpu.SemaphoreType.DMA((ncol, HB)),
            pltpu.SemaphoreType.DMA,
        ],
        compiler_params=pltpu.CompilerParams(
            collective_id=0, has_side_effects=True, vmem_limit_bytes=60 * 1024 * 1024
        ),
    )(matrix, pivots, seeds)


def solution(mesh):
    return jax.shard_map(
        local,
        mesh=mesh,
        in_specs=(P(None, "row", "col"), P(), P("col", None, None)),
        out_specs=P(None, "row", "col"),
        check_vma=False,
    )
```

```python
import functools

import jax
import jax.numpy as jnp
from jax import lax
from jax.experimental import pallas as pl
from jax.experimental.pallas import tpu as pltpu
from jax.sharding import PartitionSpec as P

HB = 8
F32 = jnp.float32
BF16 = jnp.bfloat16
MESH = pl.DeviceIdType.MESH


def split(x):
    high = x.astype(BF16)
    return high, (x - high.astype(F32)).astype(BF16)


def dot(left, right):
    return jnp.dot(left, right, preferred_element_type=F32)


def dot3(left, right):
    return dot(left[0], right[0]) + (dot(left[0], right[1]) + dot(left[1], right[0]))


def split3(x):
    high = x.astype(BF16)
    rest = x - high.astype(F32)
    middle = rest.astype(BF16)
    return high, middle, (rest - middle.astype(F32)).astype(BF16)


def kernel(
    ncol, nrow, a_hbm, piv_ref, seed_ref, out_ref,
    upper, mult, u_high, u_low, approx, x_high, x_low, e_high, e_low, f_high, f_low,
    usend, urecv, msend, mrecv, lsem, turn_sem, go_sem,
):
    square = ncol == 8 and nrow == 4 and HB >= ncol - 1
    col = lax.axis_index("col")
    row = lax.axis_index("row")
    share, width = out_ref.shape[1], out_ref.shape[2]
    first = jnp.maximum(col - HB, 0)
    chip, core = col // 2, lax.rem(col, 2)
    early = (core == 1) if square else (col < 0)
    busy = (col - core) if square else col

    middle = HB // 2 + 1
    holds = (core == 0) if square else (col < 0)

    load = pltpu.make_async_copy(a_hbm, out_ref, lsem)
    load.start()
    barrier = pltpu.get_barrier_semaphore()
    for step in range(1, nrow):
        pl.semaphore_signal(
            barrier, inc=1, device_id=(col, lax.rem(row + step, nrow)), device_id_type=MESH
        )
    for step in range(1, ncol):
        pl.semaphore_signal(
            barrier, inc=1, device_id=(lax.rem(col + step, ncol), row), device_id_type=MESH
        )
    pl.semaphore_wait(barrier, nrow + ncol - 2)
    load.wait()

    def start(copy):
        copy.start()

    def share_copy(k, slot, source, target):
        return pltpu.make_async_remote_copy(
            src_ref=upper.at[k, source],
            dst_ref=upper.at[k, source],
            send_sem=usend.at[k, slot],
            recv_sem=urecv.at[k, source],
            device_id=(col, target),
            device_id_type=MESH,
        )

    end = (row == 0) | (row == 3)
    ahead = jnp.where(row < 2, 1, -1)

    def own_sends(k, act):
        if not square:
            for step in range(1, nrow):
                act(share_copy(k, step, row, lax.rem(row + step, nrow)))
            return
        act(share_copy(k, 1, row, row + ahead))

        @pl.when(~end)
        def _():
            act(share_copy(k, 2, row, row - ahead))

    def second_sends(k, act):
        if not square:
            return

        @pl.when(end)
        def _():
            act(share_copy(k, 2, row, row + 3 * ahead))
            act(share_copy(k, 3, row, row + 2 * ahead))

        @pl.when(~end)
        def _():
            act(share_copy(k, 3, row + ahead, row - ahead))

    def start_gather(k):
        upper[k, row] = out_ref[k]
        own_sends(k, start)

    def wait_share(k, source):
        share_copy(k, 0, source, source).wait_recv()

    def relay(k):
        if square:
            wait_share(k, row + ahead)
            @pl.when((core == 1) & (k < col))
            def _():
                pl.semaphore_wait(turn_sem, 1)

            second_sends(k, start)

    def pass_turn(k):
        if square:
            @pl.when(core == 0)
            def _():
                second_sends(k, lambda copy: copy.wait_send())
                pl.semaphore_signal(turn_sem, inc=1, device_id=(col + 1, row), device_id_type=MESH)

    def sources():
        if not square:
            return [lax.rem(row + step, nrow) for step in range(1, nrow)]
        return [jnp.where(end, row + 3 * ahead, row - ahead), row + 2 * ahead]

    def finish_gather(k):
        for source in sources():
            wait_share(k, source)

    def mult_copy(k, c, slot, target):
        return pltpu.make_async_remote_copy(
            src_ref=mult.at[k, c],
            dst_ref=mult.at[k, c],
            send_sem=msend.at[k, c, slot],
            recv_sem=mrecv.at[k, c],
            device_id=(target, row),
            device_id_type=MESH,
        )

    def forward(k, c, act, near=True, far=True):
        if not square:
            @pl.when((col + 1 < ncol) & (col + 1 <= k + HB))
            def _():
                act(mult_copy(k, c, 0, col + 1))

            return
        mine = k == col
        leads = ~mine & (core == 0)
        first_part = (k == 0) & (c < middle)
        along_y = (mine & (chip < 2)) | (leads & first_part & (chip == 1))
        along_x = (mine & ((chip == 0) | (chip == 2))) | (leads & (k < 2) & ~first_part & (chip == 2))
        across = mine & (chip == 1)

        if near:
            @pl.when(core == 0)
            def _():
                act(mult_copy(k, c, 0, col + 1))

        if far:
            @pl.when(along_x | across)
            def _():
                other = jnp.where(across, 2, chip + 1 - 2 * lax.rem(chip, 2))
                act(mult_copy(k, c, 1, 2 * other))

            @pl.when(along_y)
            def _():
                act(mult_copy(k, c, 2, 2 * (chip + 2)))

    def one_hot(k):
        ordering = jnp.broadcast_to(piv_ref[pl.ds(k, 1), :], (width, width))
        hits = lax.broadcasted_iota(jnp.int32, (width, width), 0) == ordering
        return jnp.where(hits, 1.0, 0.0).astype(BF16)

    def store_swapped(k):
        ordering = piv_ref[pl.ds(k, 1), :]
        mine = ordering[:, :share]
        for other in range(1, nrow):
            mine = jnp.where(row == other, ordering[:, other * share:(other + 1) * share], mine)
        hits = lax.broadcasted_iota(jnp.int32, (width, share), 0) == jnp.broadcast_to(mine, (width, share))
        hits = jnp.where(hits, 1.0, 0.0).astype(BF16)
        parts = split3(upper[k].reshape(width, width))
        contract = (((0,), (0,)), ((), ()))
        pick = lambda part: lax.dot_general(hits, part, contract, preferred_element_type=F32)
        out_ref[k] = pick(parts[0]) + (pick(parts[1]) + pick(parts[2]))

    def split_upper(k):
        high, low = split(upper[k].reshape(width, width))
        u_high[k] = high
        u_low[k] = low

    def chunk(k, c):
        mult_copy(k, c, 0, col).wait_recv()
        forward(k, c, start)
        change = dot3(split(mult[k, c]), (u_high[k], u_low[k]))
        out_ref[k + 1 + c] = out_ref[k + 1 + c] - change

    def drain(k, carry):
        own_sends(k, lambda copy: copy.wait_send())

        @pl.when(early)
        def _():
            second_sends(k, lambda copy: copy.wait_send())

        @pl.loop(0, HB)
        def _(c):
            @pl.when(k < ncol - 1)
            def _():
                forward(k, c, lambda copy: copy.wait_send())

        return carry

    start_gather(first)

    scatter = one_hot(col)
    seed_parts = split3(seed_ref[0])
    contract = (((1,), (1,)), ((), ()))
    total = lax.dot_general(seed_parts[2], scatter, contract, preferred_element_type=F32)
    total += lax.dot_general(seed_parts[1], scatter, contract, preferred_element_type=F32)
    total += lax.dot_general(seed_parts[0], scatter, contract, preferred_element_type=F32)
    approx[...] = total
    high, low = split(total)
    x_high[...] = high
    x_low[...] = low
    relay(first)
    pass_turn(first)

    def rest(k):
        @pl.when(k >= first)
        def _():
            @pl.loop(middle, HB)
            def _(c):
                chunk(k, c)

    def update(k, carry):
        finish_gather(k)
        split_upper(k)
        chunk(k, 0)

        start_gather(k + 1)
        relay(k + 1)
        chunk(k, 1)
        pass_turn(k + 1)

        @pl.when(k + 1 < busy)
        def _():
            rest(k - 1)

            @pl.loop(2, middle)
            def _(c):
                chunk(k, c)

        store_swapped(k)
        return carry

    lax.fori_loop(first, col, update, 0)

    @pl.when(early)
    def _():
        rest(col - 3)

        @pl.when(col - 2 >= first)
        def _():
            @pl.loop(2, HB)
            def _(c):
                chunk(col - 2, c)

        @pl.when(col > first)
        def _():
            @pl.loop(2, HB)
            def _(c):
                chunk(col - 1, c)

        lax.fori_loop(first, col - 1, drain, 0)

    seed = (x_high[...], x_low[...])
    product = dot3(split(out_ref[col + 1]), seed)

    def residual(source):
        high, low = split(upper[col, source])
        rows = lax.broadcasted_iota(jnp.int32, (share, width), 0) + source * share
        unit = jnp.where(rows == lax.broadcasted_iota(jnp.int32, (share, width), 1), 1.0, 0.0)
        left = unit - dot3((high, low), (x_high[...], x_low[...]))
        high, low = split(left)
        e_high[source] = high
        e_low[source] = low

    residual(row)
    if square:
        residual(row + ahead)
    for source in sources():
        wait_share(col, source)
        residual(source)
    error = (e_high[...].reshape(width, width), e_low[...].reshape(width, width))
    product = product + dot3(split(product), error)
    mult[col, 0] = product + dot3(split(dot3(split(product), error)), error)
    forward(col, 0, start)
    if square:
        @pl.when(core == 1)
        def _():
            pl.semaphore_signal(go_sem, inc=1, device_id=(col - 1, row), device_id_type=MESH)

    error = (e_high[...].reshape(width, width), e_low[...].reshape(width, width))
    better = approx[...] + dot3((x_high[...], x_low[...]), error)
    better = better + dot3(split(better), split(dot3(error, error)))

    target = one_hot(col)
    f_high[...] = target

    @pl.when(col == ncol - 1)
    def _():
        parts = split3(better)
        swapped = dot(parts[0], target) + (dot(parts[1], target) + dot(parts[2], target))
        high, low = split(swapped)
        x_high[...] = high
        x_low[...] = low

    @pl.when(col < ncol - 1)
    def _():
        high, low = split(better)
        x_high[...] = high
        x_low[...] = low

    @pl.when(~early)
    def _():
        rest(col - 2)

    @pl.loop(1, HB)
    def _(c):
        @pl.when((col > first) & ~early & (c + 1 < HB))
        def _():
            chunk(col - 1, c + 1)

        last = dot3(split(out_ref[col + 1 + c]), (x_high[...], x_low[...]))

        @pl.when(col < ncol - 1)
        def _():
            mult[col, c] = last
            forward(col, c, start, far=False)

            @pl.when(~holds | (c < middle))
            def _():
                forward(col, c, start, near=False)

        @pl.when(col == ncol - 1)
        def _():
            out_ref[col + 1 + c] = last

    store_swapped(col)

    def permute(c):
        parts = split3(mult[col, c])
        target = f_high[...]
        out_ref[col + 1 + c] = dot(parts[0], target) + (dot(parts[1], target) + dot(parts[2], target))

    permute(0)

    @pl.when(col < ncol - 1)
    def _():
        @pl.loop(1, HB)
        def _(c):
            permute(c)

    if square:
        @pl.when(core == 0)
        def _():
            pl.semaphore_wait(go_sem, 1)

            @pl.loop(middle, HB)
            def _(c):
                forward(col, c, start, near=False)

    lax.fori_loop(jnp.where(early, jnp.maximum(first, col - 1), first), col + 1, drain, 0)


def local(matrix, pivots, seeds):
    ncol = lax.axis_size("col")
    nrow = lax.axis_size("row")
    nblk, share, width = matrix.shape
    vmem = pl.BlockSpec(memory_space=pltpu.VMEM)
    half = pltpu.VMEM((width, width), BF16)
    return pl.pallas_call(
        functools.partial(kernel, ncol, nrow),
        out_shape=jax.ShapeDtypeStruct(matrix.shape, F32),
        in_specs=[pl.BlockSpec(memory_space=pl.ANY), vmem, vmem],
        out_specs=vmem,
        scratch_shapes=[
            pltpu.VMEM((ncol, nrow, share, width), F32),
            pltpu.VMEM((ncol, HB, share, width), F32),
            pltpu.VMEM((ncol, width, width), BF16),
            pltpu.VMEM((ncol, width, width), BF16),
            pltpu.VMEM((width, width), F32),
            half,
            half,
            pltpu.VMEM((nrow, share, width), BF16),
            pltpu.VMEM((nrow, share, width), BF16),
            half,
            half,
            pltpu.SemaphoreType.DMA((ncol, nrow)),
            pltpu.SemaphoreType.DMA((ncol, nrow)),
            pltpu.SemaphoreType.DMA((ncol, HB, 3)),
            pltpu.SemaphoreType.DMA((ncol, HB)),
            pltpu.SemaphoreType.DMA,
            pltpu.SemaphoreType.REGULAR,
            pltpu.SemaphoreType.REGULAR,
        ],
        compiler_params=pltpu.CompilerParams(
            collective_id=0, has_side_effects=True, vmem_limit_bytes=60 * 1024 * 1024
        ),
    )(matrix, pivots, seeds)


def solution(mesh):
    return jax.shard_map(
        local,
        mesh=mesh,
        in_specs=(P(None, "row", "col"), P(), P("col", None, None)),
        out_specs=P(None, "row", "col"),
        check_vma=False,
    )
```

```python
import functools

import jax
import jax.numpy as jnp
from jax import lax
from jax.experimental import pallas as pl
from jax.experimental.pallas import tpu as pltpu
from jax.sharding import PartitionSpec as P

HB = 8
F32 = jnp.float32
BF16 = jnp.bfloat16
MESH = pl.DeviceIdType.MESH


def split(x):
    high = x.astype(BF16)
    return high, (x - high.astype(F32)).astype(BF16)


def dot(left, right):
    return jnp.dot(left, right, preferred_element_type=F32)


def dot3(left, right):
    return dot(left[0], right[0]) + (dot(left[0], right[1]) + dot(left[1], right[0]))


def split3(x):
    high = x.astype(BF16)
    rest = x - high.astype(F32)
    middle = rest.astype(BF16)
    return high, middle, (rest - middle.astype(F32)).astype(BF16)


def kernel(
    ncol, nrow, a_hbm, piv_ref, seed_ref, out_ref,
    upper, mult, u_high, u_low, approx, x_high, x_low, e_high, e_low, f_high, f_low,
    usend, urecv, msend, mrecv, lsem, turn_sem, go_sem,
):
    square = ncol == 8 and nrow == 4 and HB >= ncol - 1
    col = lax.axis_index("col")
    row = lax.axis_index("row")
    share, width = out_ref.shape[1], out_ref.shape[2]
    first = jnp.maximum(col - HB, 0)
    chip, core = col // 2, lax.rem(col, 2)
    early = (core == 1) if square else (col < 0)
    busy = (col - core) if square else col

    middle = HB // 2 + 1
    holds = (core == 0) if square else (col < 0)
    sent_x = jnp.where(chip == 1, 2, middle)
    thin = (chip == 2) if square else (col < 0)

    load = pltpu.make_async_copy(a_hbm, out_ref, lsem)
    load.start()
    barrier = pltpu.get_barrier_semaphore()
    for step in range(1, nrow):
        pl.semaphore_signal(
            barrier, inc=1, device_id=(col, lax.rem(row + step, nrow)), device_id_type=MESH
        )
    for step in range(1, ncol):
        pl.semaphore_signal(
            barrier, inc=1, device_id=(lax.rem(col + step, ncol), row), device_id_type=MESH
        )
    pl.semaphore_wait(barrier, nrow + ncol - 2)
    load.wait()

    def start(copy):
        copy.start()

    def share_copy(k, slot, source, target):
        return pltpu.make_async_remote_copy(
            src_ref=upper.at[k, source],
            dst_ref=upper.at[k, source],
            send_sem=usend.at[k, slot],
            recv_sem=urecv.at[k, source],
            device_id=(col, target),
            device_id_type=MESH,
        )

    end = (row == 0) | (row == 3)
    ahead = jnp.where(row < 2, 1, -1)

    def own_sends(k, act):
        if not square:
            for step in range(1, nrow):
                act(share_copy(k, step, row, lax.rem(row + step, nrow)))
            return
        act(share_copy(k, 1, row, row + ahead))

        @pl.when(~end)
        def _():
            act(share_copy(k, 2, row, row - ahead))

    def second_sends(k, act):
        if not square:
            return

        @pl.when(end)
        def _():
            act(share_copy(k, 2, row, row + 3 * ahead))
            act(share_copy(k, 3, row, row + 2 * ahead))

        @pl.when(~end)
        def _():
            act(share_copy(k, 3, row + ahead, row - ahead))

    def start_gather(k):
        upper[k, row] = out_ref[k]
        own_sends(k, start)

    def wait_share(k, source):
        share_copy(k, 0, source, source).wait_recv()

    def relay(k):
        if square:
            wait_share(k, row + ahead)
            @pl.when((core == 1) & (k < col))
            def _():
                pl.semaphore_wait(turn_sem, 1)

            second_sends(k, start)

    def pass_turn(k):
        if square:
            @pl.when(core == 0)
            def _():
                second_sends(k, lambda copy: copy.wait_send())
                pl.semaphore_signal(turn_sem, inc=1, device_id=(col + 1, row), device_id_type=MESH)

    def sources():
        if not square:
            return [lax.rem(row + step, nrow) for step in range(1, nrow)]
        return [jnp.where(end, row + 3 * ahead, row - ahead), row + 2 * ahead]

    def finish_gather(k):
        for source in sources():
            wait_share(k, source)

    def mult_copy(k, c, slot, target):
        return pltpu.make_async_remote_copy(
            src_ref=mult.at[k, c],
            dst_ref=mult.at[k, c],
            send_sem=msend.at[k, c, slot],
            recv_sem=mrecv.at[k, c],
            device_id=(target, row),
            device_id_type=MESH,
        )

    def forward(k, c, act, near=True, x=True, y=True):
        if not square:
            @pl.when((col + 1 < ncol) & (col + 1 <= k + HB))
            def _():
                act(mult_copy(k, c, 0, col + 1))

            return
        mine = k == col
        leads = ~mine & (core == 0)
        first_part = (k == 0) & (c < middle)
        along_y = (mine & (chip < 2)) | (leads & first_part & (chip == 1))
        along_x = (mine & ((chip == 0) | (chip == 2))) | (leads & (k < 2) & ~first_part & (chip == 2))
        across = mine & (chip == 1)

        if near:
            @pl.when(core == 0)
            def _():
                act(mult_copy(k, c, 0, col + 1))

        if x is not False:
            @pl.when((along_x | across) & x)
            def _():
                other = jnp.where(across, 2, chip + 1 - 2 * lax.rem(chip, 2))
                act(mult_copy(k, c, 1, 2 * other))

        if y is not False:
            @pl.when(along_y & y)
            def _():
                act(mult_copy(k, c, 2, 2 * (chip + 2)))

    def one_hot(k):
        ordering = jnp.broadcast_to(piv_ref[pl.ds(k, 1), :], (width, width))
        hits = lax.broadcasted_iota(jnp.int32, (width, width), 0) == ordering
        return jnp.where(hits, 1.0, 0.0).astype(BF16)

    def store_swapped(k):
        ordering = piv_ref[pl.ds(k, 1), :]
        mine = ordering[:, :share]
        for other in range(1, nrow):
            mine = jnp.where(row == other, ordering[:, other * share:(other + 1) * share], mine)
        hits = lax.broadcasted_iota(jnp.int32, (width, share), 0) == jnp.broadcast_to(mine, (width, share))
        hits = jnp.where(hits, 1.0, 0.0).astype(BF16)
        parts = split3(upper[k].reshape(width, width))
        contract = (((0,), (0,)), ((), ()))
        pick = lambda part: lax.dot_general(hits, part, contract, preferred_element_type=F32)
        out_ref[k] = pick(parts[0]) + (pick(parts[1]) + pick(parts[2]))

    def split_upper(k):
        high, low = split(upper[k].reshape(width, width))
        u_high[k] = high
        u_low[k] = low

    def chunk(k, c):
        mult_copy(k, c, 0, col).wait_recv()
        forward(k, c, start)
        change = dot3(split(mult[k, c]), (u_high[k], u_low[k]))
        out_ref[k + 1 + c] = out_ref[k + 1 + c] - change

    def drain(k, carry):
        own_sends(k, lambda copy: copy.wait_send())

        @pl.when(early)
        def _():
            second_sends(k, lambda copy: copy.wait_send())

        @pl.loop(0, HB)
        def _(c):
            @pl.when(k < ncol - 1)
            def _():
                forward(k, c, lambda copy: copy.wait_send())

        return carry

    start_gather(first)

    scatter = one_hot(col)
    seed_parts = split3(seed_ref[0])
    contract = (((1,), (1,)), ((), ()))
    total = lax.dot_general(seed_parts[2], scatter, contract, preferred_element_type=F32)
    total += lax.dot_general(seed_parts[1], scatter, contract, preferred_element_type=F32)
    total += lax.dot_general(seed_parts[0], scatter, contract, preferred_element_type=F32)
    approx[...] = total
    high, low = split(total)
    x_high[...] = high
    x_low[...] = low
    relay(first)
    pass_turn(first)

    def rest(k):
        @pl.when(k >= first)
        def _():
            @pl.loop(jnp.where(thin & (k == 2), 3, middle), HB)
            def _(c):
                chunk(k, c)

    def update(k, carry):
        finish_gather(k)
        split_upper(k)
        chunk(k, 0)

        start_gather(k + 1)
        relay(k + 1)
        chunk(k, 1)

        @pl.when(thin & (k == 3))
        def _():
            chunk(k - 1, 2)

        pass_turn(k + 1)

        @pl.when(k + 1 < busy)
        def _():
            rest(k - 1)

            @pl.loop(2, jnp.where(thin & (k == 2), 2, middle))
            def _(c):
                chunk(k, c)

        store_swapped(k)
        return carry

    lax.fori_loop(first, col, update, 0)

    @pl.when(early)
    def _():
        rest(col - 3)

        @pl.when(col - 2 >= first)
        def _():
            @pl.loop(2, HB)
            def _(c):
                chunk(col - 2, c)

        @pl.when(col > first)
        def _():
            @pl.loop(2, HB)
            def _(c):
                chunk(col - 1, c)

        lax.fori_loop(first, col - 1, drain, 0)

    seed = (x_high[...], x_low[...])
    product = dot3(split(out_ref[col + 1]), seed)

    def residual(source):
        high, low = split(upper[col, source])
        rows = lax.broadcasted_iota(jnp.int32, (share, width), 0) + source * share
        unit = jnp.where(rows == lax.broadcasted_iota(jnp.int32, (share, width), 1), 1.0, 0.0)
        left = unit - dot3((high, low), (x_high[...], x_low[...]))
        high, low = split(left)
        e_high[source] = high
        e_low[source] = low

    residual(row)
    if square:
        residual(row + ahead)
    for source in sources():
        wait_share(col, source)
        residual(source)
    error = (e_high[...].reshape(width, width), e_low[...].reshape(width, width))
    product = product + dot3(split(product), error)
    mult[col, 0] = product + dot3(split(dot3(split(product), error)), error)
    forward(col, 0, start)
    if square:
        @pl.when(core == 1)
        def _():
            pl.semaphore_signal(go_sem, inc=1, device_id=(col - 1, row), device_id_type=MESH)

    error = (e_high[...].reshape(width, width), e_low[...].reshape(width, width))
    better = approx[...] + dot3((x_high[...], x_low[...]), error)
    better = better + dot3(split(better), split(dot3(error, error)))

    target = one_hot(col)
    f_high[...] = target

    @pl.when(col == ncol - 1)
    def _():
        parts = split3(better)
        swapped = dot(parts[0], target) + (dot(parts[1], target) + dot(parts[2], target))
        high, low = split(swapped)
        x_high[...] = high
        x_low[...] = low

    @pl.when(col < ncol - 1)
    def _():
        high, low = split(better)
        x_high[...] = high
        x_low[...] = low

    @pl.when(~early)
    def _():
        rest(col - 2)

    @pl.loop(1, HB)
    def _(c):
        @pl.when((col > first) & ~early & (c + 1 < HB))
        def _():
            chunk(col - 1, c + 1)

        last = dot3(split(out_ref[col + 1 + c]), (x_high[...], x_low[...]))

        @pl.when(col < ncol - 1)
        def _():
            mult[col, c] = last
            forward(col, c, start, x=~holds | (c < sent_x), y=~holds | (c < middle))

        @pl.when(col == ncol - 1)
        def _():
            out_ref[col + 1 + c] = last

    store_swapped(col)

    def permute(c):
        parts = split3(mult[col, c])
        target = f_high[...]
        out_ref[col + 1 + c] = dot(parts[0], target) + (dot(parts[1], target) + dot(parts[2], target))

    permute(0)

    @pl.when(col < ncol - 1)
    def _():
        @pl.loop(1, HB)
        def _(c):
            permute(c)

    if square:
        @pl.when(core == 0)
        def _():
            pl.semaphore_wait(go_sem, 1)

            @pl.loop(2, HB)
            def _(c):
                forward(col, c, start, near=False, x=c >= sent_x, y=c >= middle)

    lax.fori_loop(jnp.where(early, jnp.maximum(first, col - 1), first), col + 1, drain, 0)


def local(matrix, pivots, seeds):
    ncol = lax.axis_size("col")
    nrow = lax.axis_size("row")
    nblk, share, width = matrix.shape
    vmem = pl.BlockSpec(memory_space=pltpu.VMEM)
    half = pltpu.VMEM((width, width), BF16)
    words = 2 * nblk * share * width + ncol * width * width * 2 + ncol * HB * share * width + 6 * width * width
    limit = min(4 * words + 2**20, 60 * 1024 * 1024)
    return pl.pallas_call(
        functools.partial(kernel, ncol, nrow),
        out_shape=jax.ShapeDtypeStruct(matrix.shape, F32),
        in_specs=[pl.BlockSpec(memory_space=pl.ANY), vmem, vmem],
        out_specs=vmem,
        scratch_shapes=[
            pltpu.VMEM((ncol, nrow, share, width), F32),
            pltpu.VMEM((ncol, HB, share, width), F32),
            pltpu.VMEM((ncol, width, width), BF16),
            pltpu.VMEM((ncol, width, width), BF16),
            pltpu.VMEM((width, width), F32),
            half,
            half,
            pltpu.VMEM((nrow, share, width), BF16),
            pltpu.VMEM((nrow, share, width), BF16),
            half,
            half,
            pltpu.SemaphoreType.DMA((ncol, nrow)),
            pltpu.SemaphoreType.DMA((ncol, nrow)),
            pltpu.SemaphoreType.DMA((ncol, HB, 3)),
            pltpu.SemaphoreType.DMA((ncol, HB)),
            pltpu.SemaphoreType.DMA,
            pltpu.SemaphoreType.REGULAR,
            pltpu.SemaphoreType.REGULAR,
        ],
        compiler_params=pltpu.CompilerParams(
            collective_id=0, has_side_effects=True, vmem_limit_bytes=limit
        ),
    )(matrix, pivots, seeds)


def solution(mesh):
    return jax.shard_map(
        local,
        mesh=mesh,
        in_specs=(P(None, "row", "col"), P(), P("col", None, None)),
        out_specs=P(None, "row", "col"),
        check_vma=False,
    )
```

```python
import functools

import jax
import jax.numpy as jnp
from jax import lax
from jax.experimental import pallas as pl
from jax.experimental.pallas import tpu as pltpu
from jax.sharding import PartitionSpec as P

HB = 8
F32 = jnp.float32
BF16 = jnp.bfloat16
MESH = pl.DeviceIdType.MESH


def split(x):
    high = x.astype(BF16)
    return high, (x - high.astype(F32)).astype(BF16)


def dot(left, right):
    return jnp.dot(left, right, preferred_element_type=F32)


def dot3(left, right):
    return dot(left[0], right[0]) + (dot(left[0], right[1]) + dot(left[1], right[0]))


def split3(x):
    high = x.astype(BF16)
    rest = x - high.astype(F32)
    middle = rest.astype(BF16)
    return high, middle, (rest - middle.astype(F32)).astype(BF16)


def kernel(
    ncol, nrow, a_hbm, piv_ref, seed_ref, out_any,
    work, upper, mult, u_high, u_low, approx, x_high, x_low, e_high, e_low, f_high, f_low,
    usend, urecv, msend, mrecv, lsem, turn_sem, go_sem, osem,
):
    square = ncol == 8 and nrow == 4 and HB >= ncol - 1
    col = lax.axis_index("col")
    row = lax.axis_index("row")
    share, width = work.shape[1], work.shape[2]
    first = jnp.maximum(col - HB, 0)
    chip, core = col // 2, lax.rem(col, 2)
    early = (core == 1) if square else (col < 0)
    busy = (col - core) if square else col
    final = early & (col == ncol - 1)

    middle = HB // 2 + 1
    holds = (core == 0) if square else (col < 0)
    sent_x = jnp.where(chip == 1, 2, middle)
    thin = (chip == 2) if square else (col < 0)

    load = pltpu.make_async_copy(a_hbm, work, lsem)
    load.start()
    barrier = pltpu.get_barrier_semaphore()
    for step in range(1, nrow):
        pl.semaphore_signal(
            barrier, inc=1, device_id=(col, lax.rem(row + step, nrow)), device_id_type=MESH
        )
    for step in range(1, ncol):
        pl.semaphore_signal(
            barrier, inc=1, device_id=(lax.rem(col + step, ncol), row), device_id_type=MESH
        )
    pl.semaphore_wait(barrier, nrow + ncol - 2)
    load.wait()

    def row_out(r):
        return pltpu.make_async_copy(work.at[r], out_any.at[r], osem.at[r])

    @pl.loop(0, first)
    def _(r):
        row_out(r).start()

    @pl.loop(col + HB + 1, work.shape[0])
    def _(r):
        row_out(r).start()


    def start(copy):
        copy.start()

    def share_copy(k, slot, source, target):
        return pltpu.make_async_remote_copy(
            src_ref=upper.at[k, source],
            dst_ref=upper.at[k, source],
            send_sem=usend.at[k, slot],
            recv_sem=urecv.at[k, source],
            device_id=(col, target),
            device_id_type=MESH,
        )

    end = (row == 0) | (row == 3)
    ahead = jnp.where(row < 2, 1, -1)

    def own_sends(k, act):
        if not square:
            for step in range(1, nrow):
                act(share_copy(k, step, row, lax.rem(row + step, nrow)))
            return
        act(share_copy(k, 1, row, row + ahead))

        @pl.when(~end)
        def _():
            act(share_copy(k, 2, row, row - ahead))

    def second_sends(k, act, far=True):
        if not square:
            return

        @pl.when(end)
        def _():
            if far:
                act(share_copy(k, 2, row, row + 3 * ahead))
            act(share_copy(k, 3, row, row + 2 * ahead))

        @pl.when(~end)
        def _():
            act(share_copy(k, 3, row + ahead, row - ahead))

    def start_gather(k):
        upper[k, row] = work[k]
        own_sends(k, start)

    def wait_share(k, source):
        share_copy(k, 0, source, source).wait_recv()

    def relay(k):
        if square:
            wait_share(k, row + ahead)
            @pl.when((core == 1) & (k < col))
            def _():
                pl.semaphore_wait(turn_sem, 1)

            second_sends(k, start)

    def pass_turn(k):
        if square:
            @pl.when(core == 0)
            def _():
                @pl.when(end)
                def _():
                    share_copy(k, 2, row, row + 3 * ahead).wait_send()

                pl.semaphore_signal(turn_sem, inc=1, device_id=(col + 1, row), device_id_type=MESH)

    def sources():
        if not square:
            return [lax.rem(row + step, nrow) for step in range(1, nrow)]
        return [jnp.where(end, row + 3 * ahead, row - ahead), row + 2 * ahead]

    def finish_gather(k):
        for source in sources():
            wait_share(k, source)

    def mult_copy(k, c, slot, target):
        return pltpu.make_async_remote_copy(
            src_ref=mult.at[k, c],
            dst_ref=mult.at[k, c],
            send_sem=msend.at[k, c, slot],
            recv_sem=mrecv.at[k, c],
            device_id=(target, row),
            device_id_type=MESH,
        )

    def forward(k, c, act, near=True, x=True, y=True):
        if not square:
            @pl.when((col + 1 < ncol) & (col + 1 <= k + HB))
            def _():
                act(mult_copy(k, c, 0, col + 1))

            return
        mine = k == col
        leads = ~mine & (core == 0)
        first_part = (k == 0) & (c < middle)
        along_y = (mine & (chip < 2)) | (leads & first_part & (chip == 1))
        along_x = (mine & ((chip == 0) | (chip == 2))) | (leads & (k < 2) & ~first_part & (chip == 2))
        across = mine & (chip == 1)

        if near:
            @pl.when(core == 0)
            def _():
                act(mult_copy(k, c, 0, col + 1))

        if x is not False:
            @pl.when((along_x | across) & x)
            def _():
                other = jnp.where(across, 2, chip + 1 - 2 * lax.rem(chip, 2))
                act(mult_copy(k, c, 1, 2 * other))

        if y is not False:
            @pl.when(along_y & y)
            def _():
                act(mult_copy(k, c, 2, 2 * (chip + 2)))

    def one_hot(k):
        ordering = jnp.broadcast_to(piv_ref[pl.ds(k, 1), :], (width, width))
        hits = lax.broadcasted_iota(jnp.int32, (width, width), 0) == ordering
        return jnp.where(hits, 1.0, 0.0).astype(BF16)

    def store_swapped(k):
        ordering = piv_ref[pl.ds(k, 1), :]
        mine = ordering[:, :share]
        for other in range(1, nrow):
            mine = jnp.where(row == other, ordering[:, other * share:(other + 1) * share], mine)
        hits = lax.broadcasted_iota(jnp.int32, (width, share), 0) == jnp.broadcast_to(mine, (width, share))
        hits = jnp.where(hits, 1.0, 0.0).astype(BF16)
        parts = split3(upper[k].reshape(width, width))
        contract = (((0,), (0,)), ((), ()))
        pick = lambda part: lax.dot_general(hits, part, contract, preferred_element_type=F32)
        work[k] = pick(parts[0]) + (pick(parts[1]) + pick(parts[2]))
        row_out(k).start()

    def split_upper(k):
        high, low = split(upper[k].reshape(width, width))
        u_high[k] = high
        u_low[k] = low

    def chunk(k, c):
        mult_copy(k, c, 0, col).wait_recv()
        forward(k, c, start)
        change = dot3(split(mult[k, c]), (u_high[k], u_low[k]))
        work[k + 1 + c] = work[k + 1 + c] - change

    def drain(k, carry):
        own_sends(k, lambda copy: copy.wait_send())

        second_sends(k, lambda copy: copy.wait_send(), far=False)

        @pl.when(early & end)
        def _():
            share_copy(k, 2, row, row + 3 * ahead).wait_send()

        @pl.loop(0, HB)
        def _(c):
            @pl.when(k < ncol - 1)
            def _():
                forward(k, c, lambda copy: copy.wait_send())

        return carry

    start_gather(first)

    scatter = one_hot(col)
    seed_parts = split3(seed_ref[0])
    contract = (((1,), (1,)), ((), ()))
    total = lax.dot_general(seed_parts[2], scatter, contract, preferred_element_type=F32)
    total += lax.dot_general(seed_parts[1], scatter, contract, preferred_element_type=F32)
    total += lax.dot_general(seed_parts[0], scatter, contract, preferred_element_type=F32)
    approx[...] = total
    high, low = split(total)
    x_high[...] = high
    x_low[...] = low
    relay(first)

    @pl.when(first < col)
    def _():
        pass_turn(first)

    def rest(k, skip=0):
        @pl.when(k >= first)
        def _():
            @pl.loop(jnp.where(thin & (k == 2), 3 + skip, middle), HB)
            def _(c):
                chunk(k, c)

    def update(k, carry):
        finish_gather(k)
        split_upper(k)
        chunk(k, 0)

        start_gather(k + 1)
        relay(k + 1)
        chunk(k, 1)

        @pl.when(thin & (k == 3))
        def _():
            chunk(k - 1, 2)

        @pl.when(k + 1 < col)
        def _():
            pass_turn(k + 1)

        @pl.when(k + 1 < busy)
        def _():
            rest(k - 1)

            @pl.loop(2, jnp.where(thin & (k == 2), 2, middle))
            def _(c):
                chunk(k, c)

        store_swapped(k)
        return carry

    lax.fori_loop(first, col, update, 0)

    def overdue(skip):
        rest(col - 3, skip)

        @pl.when(col - 2 >= first)
        def _():
            @pl.loop(2 + skip, HB)
            def _(c):
                chunk(col - 2, c)

        @pl.when(col > first)
        def _():
            @pl.loop(2, HB)
            def _(c):
                chunk(col - 1, c)

    @pl.when(early & ~final & (col - 2 >= first))
    def _():
        chunk(col - 2, 2)

        @pl.when(thin & (col == 5))
        def _():
            chunk(col - 3, 3)

    @pl.when(final)
    def _():
        overdue(0)
        lax.fori_loop(first, col - 1, drain, 0)

    seed = (x_high[...], x_low[...])
    product = dot3(split(work[col + 1]), seed)

    def residual(source):
        high, low = split(upper[col, source])
        rows = lax.broadcasted_iota(jnp.int32, (share, width), 0) + source * share
        unit = jnp.where(rows == lax.broadcasted_iota(jnp.int32, (share, width), 1), 1.0, 0.0)
        left = unit - dot3((high, low), (x_high[...], x_low[...]))
        high, low = split(left)
        e_high[source] = high
        e_low[source] = low

    residual(row)
    if square:
        residual(row + ahead)
    pass_turn(col)
    for source in sources():
        wait_share(col, source)
        residual(source)
    error = (e_high[...].reshape(width, width), e_low[...].reshape(width, width))
    product = product + dot3(split(product), error)
    mult[col, 0] = product + dot3(split(dot3(split(product), error)), error)
    forward(col, 0, start)
    if square:
        @pl.when(core == 1)
        def _():
            pl.semaphore_signal(go_sem, inc=1, device_id=(col - 1, row), device_id_type=MESH)

    error = (e_high[...].reshape(width, width), e_low[...].reshape(width, width))
    better = approx[...] + dot3((x_high[...], x_low[...]), error)
    better = better + dot3(split(better), split(dot3(error, error)))

    target = one_hot(col)
    f_high[...] = target

    @pl.when(col == ncol - 1)
    def _():
        parts = split3(better)
        swapped = dot(parts[0], target) + (dot(parts[1], target) + dot(parts[2], target))
        high, low = split(swapped)
        x_high[...] = high
        x_low[...] = low

    @pl.when(col < ncol - 1)
    def _():
        high, low = split(better)
        x_high[...] = high
        x_low[...] = low

    @pl.when(~early)
    def _():
        rest(col - 2)

    @pl.when(early & ~final)
    def _():
        overdue(1)

    @pl.loop(1, HB)
    def _(c):
        @pl.when((col > first) & ~early & (c + 1 < HB))
        def _():
            chunk(col - 1, c + 1)

        last = dot3(split(work[col + 1 + c]), (x_high[...], x_low[...]))

        @pl.when(col < ncol - 1)
        def _():
            mult[col, c] = last
            forward(col, c, start, x=~holds | (c < sent_x), y=~holds | (c < middle))

        @pl.when(col == ncol - 1)
        def _():
            work[col + 1 + c] = last
            row_out(col + 1 + c).start()

    store_swapped(col)

    def permute(c):
        parts = split3(mult[col, c])
        target = f_high[...]
        work[col + 1 + c] = dot(parts[0], target) + (dot(parts[1], target) + dot(parts[2], target))
        row_out(col + 1 + c).start()

    permute(0)

    @pl.when(col < ncol - 1)
    def _():
        @pl.loop(1, HB)
        def _(c):
            permute(c)

    if square:
        @pl.when(core == 0)
        def _():
            pl.semaphore_wait(go_sem, 1)

            @pl.loop(2, HB)
            def _(c):
                forward(col, c, start, near=False, x=c >= sent_x, y=c >= middle)

    lax.fori_loop(jnp.where(final, jnp.maximum(first, col - 1), first), col + 1, drain, 0)

    @pl.loop(0, work.shape[0])
    def _(r):
        row_out(r).wait()


def local(matrix, pivots, seeds):
    ncol = lax.axis_size("col")
    nrow = lax.axis_size("row")
    nblk, share, width = matrix.shape
    vmem = pl.BlockSpec(memory_space=pltpu.VMEM)
    half = pltpu.VMEM((width, width), BF16)
    words = 2 * nblk * share * width + ncol * width * width * 2 + ncol * HB * share * width + 6 * width * width
    limit = min(4 * words + 2**20, 60 * 1024 * 1024)
    return pl.pallas_call(
        functools.partial(kernel, ncol, nrow),
        out_shape=jax.ShapeDtypeStruct(matrix.shape, F32),
        in_specs=[pl.BlockSpec(memory_space=pl.ANY), vmem, vmem],
        out_specs=pl.BlockSpec(memory_space=pl.ANY),
        scratch_shapes=[
            pltpu.VMEM(matrix.shape, F32),
            pltpu.VMEM((ncol, nrow, share, width), F32),
            pltpu.VMEM((ncol, HB, share, width), F32),
            pltpu.VMEM((ncol, width, width), BF16),
            pltpu.VMEM((ncol, width, width), BF16),
            pltpu.VMEM((width, width), F32),
            half,
            half,
            pltpu.VMEM((nrow, share, width), BF16),
            pltpu.VMEM((nrow, share, width), BF16),
            half,
            half,
            pltpu.SemaphoreType.DMA((ncol, nrow)),
            pltpu.SemaphoreType.DMA((ncol, nrow)),
            pltpu.SemaphoreType.DMA((ncol, HB, 3)),
            pltpu.SemaphoreType.DMA((ncol, HB)),
            pltpu.SemaphoreType.DMA,
            pltpu.SemaphoreType.REGULAR,
            pltpu.SemaphoreType.REGULAR,
            pltpu.SemaphoreType.DMA((nblk,)),
        ],
        compiler_params=pltpu.CompilerParams(
            collective_id=0, has_side_effects=True, vmem_limit_bytes=limit
        ),
    )(matrix, pivots, seeds)


def solution(mesh):
    return jax.shard_map(
        local,
        mesh=mesh,
        in_specs=(P(None, "row", "col"), P(), P("col", None, None)),
        out_specs=P(None, "row", "col"),
        check_vma=False,
    )
```

```python
import functools

import jax
import jax.numpy as jnp
from jax import lax
from jax.experimental import pallas as pl
from jax.experimental.pallas import tpu as pltpu
from jax.sharding import PartitionSpec as P

HB = 8
F32 = jnp.float32
BF16 = jnp.bfloat16
MESH = pl.DeviceIdType.MESH


def split(x):
    high = x.astype(BF16)
    return high, (x - high.astype(F32)).astype(BF16)


def dot(left, right):
    return jnp.dot(left, right, preferred_element_type=F32)


def dot3(left, right):
    return dot(left[0], right[0]) + (dot(left[0], right[1]) + dot(left[1], right[0]))


def split3(x):
    high = x.astype(BF16)
    rest = x - high.astype(F32)
    middle = rest.astype(BF16)
    return high, middle, (rest - middle.astype(F32)).astype(BF16)


def kernel(
    ncol, nrow, a_hbm, piv_any, seed_any, out_any,
    piv_ref, work, upper, mult, u_high, u_low, approx, x_high, x_low, e_high, e_low, order,
    usend, urecv, msend, mrecv, lsem, turn_sem, go_sem, osem,
):
    square = ncol == 8 and nrow == 4 and HB >= ncol - 1
    col = lax.axis_index("col")
    row = lax.axis_index("row")
    share, width = work.shape[1], work.shape[2]
    first = jnp.maximum(col - HB, 0)
    chip, core = col // 2, lax.rem(col, 2)
    early = (core == 1) if square else (col < 0)
    busy = (col - core) if square else col
    final = early & (col == ncol - 1)

    middle = HB // 2 + 1
    holds = (core == 0) if square else (col < 0)
    sent_x = jnp.where(chip == 1, 2, middle)
    thin = (chip == 2) if square else (col < 0)

    load = pltpu.make_async_copy(a_hbm, work, lsem.at[0])
    load_pivots = pltpu.make_async_copy(piv_any, piv_ref, lsem.at[1])
    load_seed = pltpu.make_async_copy(seed_any.at[0], approx, lsem.at[2])
    for copy in (load, load_pivots, load_seed):
        copy.start()
    barrier = pltpu.get_barrier_semaphore()
    for step in range(1, nrow):
        pl.semaphore_signal(
            barrier, inc=1, device_id=(col, lax.rem(row + step, nrow)), device_id_type=MESH
        )
    for step in range(1, ncol):
        pl.semaphore_signal(
            barrier, inc=1, device_id=(lax.rem(col + step, ncol), row), device_id_type=MESH
        )
    pl.semaphore_wait(barrier, nrow + ncol - 2)
    load.wait()

    def row_out(r):
        return pltpu.make_async_copy(work.at[r], out_any.at[r], osem.at[r])

    @pl.loop(0, first)
    def _(r):
        row_out(r).start()

    @pl.loop(col + HB + 1, work.shape[0])
    def _(r):
        row_out(r).start()


    def start(copy):
        copy.start()

    def share_copy(k, slot, source, target):
        return pltpu.make_async_remote_copy(
            src_ref=upper.at[k, source],
            dst_ref=upper.at[k, source],
            send_sem=usend.at[k, slot],
            recv_sem=urecv.at[k, source],
            device_id=(col, target),
            device_id_type=MESH,
        )

    end = (row == 0) | (row == 3)
    ahead = jnp.where(row < 2, 1, -1)

    def own_sends(k, act):
        if not square:
            for step in range(1, nrow):
                act(share_copy(k, step, row, lax.rem(row + step, nrow)))
            return
        act(share_copy(k, 1, row, row + ahead))

        @pl.when(~end)
        def _():
            act(share_copy(k, 2, row, row - ahead))

    def second_sends(k, act, far=True):
        if not square:
            return

        @pl.when(end)
        def _():
            if far:
                act(share_copy(k, 2, row, row + 3 * ahead))
            act(share_copy(k, 3, row, row + 2 * ahead))

        @pl.when(~end)
        def _():
            act(share_copy(k, 3, row + ahead, row - ahead))

    def start_gather(k):
        upper[k, row] = work[k]
        own_sends(k, start)

    def wait_share(k, source):
        share_copy(k, 0, source, source).wait_recv()

    def relay(k):
        if square:
            wait_share(k, row + ahead)
            @pl.when((core == 1) & (k < col))
            def _():
                pl.semaphore_wait(turn_sem, 1)

            second_sends(k, start)

    def pass_turn(k):
        if square:
            @pl.when(core == 0)
            def _():
                @pl.when(end)
                def _():
                    share_copy(k, 2, row, row + 3 * ahead).wait_send()

                pl.semaphore_signal(turn_sem, inc=1, device_id=(col + 1, row), device_id_type=MESH)

    def sources():
        if not square:
            return [lax.rem(row + step, nrow) for step in range(1, nrow)]
        return [jnp.where(end, row + 3 * ahead, row - ahead), row + 2 * ahead]

    def finish_gather(k):
        for source in sources():
            wait_share(k, source)

    def mult_copy(k, c, slot, target):
        return pltpu.make_async_remote_copy(
            src_ref=mult.at[k, c],
            dst_ref=mult.at[k, c],
            send_sem=msend.at[k, c, slot],
            recv_sem=mrecv.at[k, c],
            device_id=(target, row),
            device_id_type=MESH,
        )

    def forward(k, c, act, near=True, x=True, y=True):
        if not square:
            @pl.when((col + 1 < ncol) & (col + 1 <= k + HB))
            def _():
                act(mult_copy(k, c, 0, col + 1))

            return
        mine = k == col
        leads = ~mine & (core == 0)
        first_part = (k == 0) & (c < middle)
        along_y = (mine & (chip < 2)) | (leads & first_part & (chip == 1))
        along_x = (mine & ((chip == 0) | (chip == 2))) | (leads & (k < 2) & ~first_part & (chip == 2))
        across = mine & (chip == 1)

        if near:
            @pl.when(core == 0)
            def _():
                act(mult_copy(k, c, 0, col + 1))

        if x is not False:
            @pl.when((along_x | across) & x)
            def _():
                other = jnp.where(across, 2, chip + 1 - 2 * lax.rem(chip, 2))
                act(mult_copy(k, c, 1, 2 * other))

        if y is not False:
            @pl.when(along_y & y)
            def _():
                act(mult_copy(k, c, 2, 2 * (chip + 2)))

    def one_hot(k):
        ordering = jnp.broadcast_to(piv_ref[pl.ds(k, 1), :], (width, width))
        hits = lax.broadcasted_iota(jnp.int32, (width, width), 0) == ordering
        return jnp.where(hits, 1.0, 0.0).astype(BF16)

    def store_swapped(k):
        ordering = piv_ref[pl.ds(k, 1), :]
        mine = ordering[:, :share]
        for other in range(1, nrow):
            mine = jnp.where(row == other, ordering[:, other * share:(other + 1) * share], mine)
        hits = lax.broadcasted_iota(jnp.int32, (width, share), 0) == jnp.broadcast_to(mine, (width, share))
        hits = jnp.where(hits, 1.0, 0.0).astype(BF16)
        parts = split3(upper[k].reshape(width, width))
        contract = (((0,), (0,)), ((), ()))
        pick = lambda part: lax.dot_general(hits, part, contract, preferred_element_type=F32)
        work[k] = pick(parts[0]) + (pick(parts[1]) + pick(parts[2]))
        row_out(k).start()

    def split_upper(k):
        high, low = split(upper[k].reshape(width, width))
        u_high[k] = high
        u_low[k] = low

    def chunk(k, c):
        mult_copy(k, c, 0, col).wait_recv()
        forward(k, c, start)
        change = dot3(split(mult[k, c]), (u_high[k], u_low[k]))
        work[k + 1 + c] = work[k + 1 + c] - change

    def drain(k, carry):
        own_sends(k, lambda copy: copy.wait_send())

        second_sends(k, lambda copy: copy.wait_send(), far=False)

        @pl.when(early & end)
        def _():
            share_copy(k, 2, row, row + 3 * ahead).wait_send()

        @pl.loop(0, HB)
        def _(c):
            @pl.when(k < ncol - 1)
            def _():
                forward(k, c, lambda copy: copy.wait_send())

        return carry

    start_gather(first)

    load_pivots.wait()
    scatter = one_hot(col)
    order[...] = scatter
    load_seed.wait()
    seed_parts = split3(approx[...])
    contract = (((1,), (1,)), ((), ()))
    total = lax.dot_general(seed_parts[2], scatter, contract, preferred_element_type=F32)
    total += lax.dot_general(seed_parts[1], scatter, contract, preferred_element_type=F32)
    total += lax.dot_general(seed_parts[0], scatter, contract, preferred_element_type=F32)
    approx[...] = total
    high, low = split(total)
    x_high[...] = high
    x_low[...] = low
    relay(first)

    @pl.when(first < col)
    def _():
        pass_turn(first)

    def rest(k, skip=0):
        @pl.when(k >= first)
        def _():
            @pl.loop(jnp.where(thin & (k == 2), 3 + skip, middle), HB)
            def _(c):
                chunk(k, c)

    def update(k, carry):
        finish_gather(k)
        split_upper(k)
        chunk(k, 0)

        start_gather(k + 1)
        relay(k + 1)
        chunk(k, 1)

        @pl.when(thin & (k == 3))
        def _():
            chunk(k - 1, 2)

        @pl.when(k + 1 < col)
        def _():
            pass_turn(k + 1)

        @pl.when(k + 1 < busy)
        def _():
            rest(k - 1)

            @pl.loop(2, jnp.where(thin & (k == 2), 2, middle))
            def _(c):
                chunk(k, c)

        store_swapped(k)
        return carry

    lax.fori_loop(first, col, update, 0)

    def overdue(skip):
        rest(col - 3, skip)

        @pl.when(col - 2 >= first)
        def _():
            @pl.loop(2 + skip, HB)
            def _(c):
                chunk(col - 2, c)

        @pl.when(col > first)
        def _():
            @pl.loop(2, HB)
            def _(c):
                chunk(col - 1, c)

    @pl.when(early & ~final & (col - 2 >= first))
    def _():
        chunk(col - 2, 2)

        @pl.when(thin & (col == 5))
        def _():
            chunk(col - 3, 3)

    @pl.when(final)
    def _():
        overdue(0)
        lax.fori_loop(first, col - 1, drain, 0)

    seed = (x_high[...], x_low[...])
    mult[col, 0] = dot3(split(work[col + 1]), seed)

    def residual(source):
        high, low = split(upper[col, source])
        rows = lax.broadcasted_iota(jnp.int32, (share, width), 0) + source * share
        unit = jnp.where(rows == lax.broadcasted_iota(jnp.int32, (share, width), 1), 1.0, 0.0)
        left = unit - dot3((high, low), (x_high[...], x_low[...]))
        high, low = split(left)
        e_high[source] = high
        e_low[source] = low

    residual(row)
    if square:
        residual(row + ahead)
    pass_turn(col)
    for source in sources():
        wait_share(col, source)
        residual(source)
    error = (e_high[...].reshape(width, width), e_low[...].reshape(width, width))

    @pl.when(col < ncol - 1)
    def _():
        product = mult[col, 0]
        product = product + dot3(split(product), error)
        mult[col, 0] = product + dot3(split(dot3(split(product), error)), error)
        forward(col, 0, start)

    if square:
        @pl.when(core == 1)
        def _():
            pl.semaphore_signal(go_sem, inc=1, device_id=(col - 1, row), device_id_type=MESH)

    error = (e_high[...].reshape(width, width), e_low[...].reshape(width, width))
    better = approx[...] + dot3((x_high[...], x_low[...]), error)
    better = better + dot3(split(better), split(dot3(error, error)))

    high, low = split(better)

    @pl.when(col == ncol - 1)
    def _():
        target = order[...]
        x_high[...] = dot(high, target).astype(BF16)
        x_low[...] = dot(low, target).astype(BF16)

    @pl.when(col < ncol - 1)
    def _():
        x_high[...] = high
        x_low[...] = low

    @pl.when(~early)
    def _():
        rest(col - 2)

    @pl.when(early & ~final)
    def _():
        overdue(1)

    @pl.loop(jnp.where(col < ncol - 1, 1, 0), HB)
    def _(c):
        @pl.when((col > first) & ~early & (c > 0) & (c + 1 < HB))
        def _():
            chunk(col - 1, c + 1)

        last = dot3(split(work[col + 1 + c]), (x_high[...], x_low[...]))

        @pl.when(col < ncol - 1)
        def _():
            mult[col, c] = last
            forward(col, c, start, x=~holds | (c < sent_x), y=~holds | (c < middle))

        @pl.when(col == ncol - 1)
        def _():
            work[col + 1 + c] = last
            row_out(col + 1 + c).start()

    store_swapped(col)

    def permute(c):
        parts = split3(mult[col, c])
        target = order[...]
        work[col + 1 + c] = dot(parts[0], target) + (dot(parts[1], target) + dot(parts[2], target))
        row_out(col + 1 + c).start()

    @pl.when(col < ncol - 1)
    def _():
        @pl.loop(0, HB)
        def _(c):
            permute(c)

    if square:
        @pl.when(core == 0)
        def _():
            pl.semaphore_wait(go_sem, 1)

            @pl.loop(2, HB)
            def _(c):
                forward(col, c, start, near=False, x=c >= sent_x, y=c >= middle)

    lax.fori_loop(jnp.where(final, jnp.maximum(first, col - 1), first), col + 1, drain, 0)

    @pl.loop(0, work.shape[0])
    def _(r):
        row_out(r).wait()


def local(matrix, pivots, seeds):
    ncol = lax.axis_size("col")
    nrow = lax.axis_size("row")
    nblk, share, width = matrix.shape
    anywhere = pl.BlockSpec(memory_space=pl.ANY)
    half = pltpu.VMEM((width, width), BF16)
    words = 2 * nblk * share * width + ncol * width * width * 2 + ncol * HB * share * width + 6 * width * width
    limit = min(4 * words + 2**20, 60 * 1024 * 1024)
    return pl.pallas_call(
        functools.partial(kernel, ncol, nrow),
        out_shape=jax.ShapeDtypeStruct(matrix.shape, F32),
        in_specs=[anywhere] * 3,
        out_specs=anywhere,
        scratch_shapes=[
            pltpu.VMEM(pivots.shape, jnp.int32),
            pltpu.VMEM(matrix.shape, F32),
            pltpu.VMEM((ncol, nrow, share, width), F32),
            pltpu.VMEM((ncol, HB, share, width), F32),
            pltpu.VMEM((ncol, width, width), BF16),
            pltpu.VMEM((ncol, width, width), BF16),
            pltpu.VMEM((width, width), F32),
            half,
            half,
            pltpu.VMEM((nrow, share, width), BF16),
            pltpu.VMEM((nrow, share, width), BF16),
            half,
            pltpu.SemaphoreType.DMA((ncol, nrow)),
            pltpu.SemaphoreType.DMA((ncol, nrow)),
            pltpu.SemaphoreType.DMA((ncol, HB, 3)),
            pltpu.SemaphoreType.DMA((ncol, HB)),
            pltpu.SemaphoreType.DMA((3,)),
            pltpu.SemaphoreType.REGULAR,
            pltpu.SemaphoreType.REGULAR,
            pltpu.SemaphoreType.DMA((nblk,)),
        ],
        compiler_params=pltpu.CompilerParams(
            collective_id=0, has_side_effects=True, vmem_limit_bytes=limit
        ),
    )(matrix, pivots, seeds)


def solution(mesh):
    return jax.shard_map(
        local,
        mesh=mesh,
        in_specs=(P(None, "row", "col"), P(), P("col", None, None)),
        out_specs=P(None, "row", "col"),
        check_vma=False,
    )
```

```python
import functools

import jax
import jax.numpy as jnp
from jax import lax
from jax.experimental import pallas as pl
from jax.experimental.pallas import tpu as pltpu
from jax.sharding import PartitionSpec as P

HB = 8
F32 = jnp.float32
BF16 = jnp.bfloat16
MESH = pl.DeviceIdType.MESH


def split(x):
    high = x.astype(BF16)
    return high, (x - high.astype(F32)).astype(BF16)


def dot(left, right):
    return jnp.dot(left, right, preferred_element_type=F32)


def dot3(left, right):
    return dot(left[0], right[0]) + (dot(left[0], right[1]) + dot(left[1], right[0]))


def split3(x):
    high = x.astype(BF16)
    rest = x - high.astype(F32)
    middle = rest.astype(BF16)
    return high, middle, (rest - middle.astype(F32)).astype(BF16)


def kernel(
    ncol, nrow, a_hbm, piv_any, seed_any, out_any,
    piv_ref, work, upper, mult, u_high, u_low, approx, x_high, x_low, e_high, e_low, order,
    usend, urecv, msend, mrecv, lsem, turn_sem, go_sem, osem,
):
    square = ncol == 8 and nrow == 4 and HB >= ncol - 1
    col = lax.axis_index("col")
    row = lax.axis_index("row")
    share, width = work.shape[1], work.shape[2]
    first = jnp.maximum(col - HB, 0)
    chip, core = col // 2, lax.rem(col, 2)
    early = (core == 1) if square else (col < 0)
    busy = (col - core) if square else col
    final = early & (col == ncol - 1)

    middle = HB // 2 + 1
    holds = (core == 0) if square else (col < 0)
    sent_x = jnp.where(chip == 1, 3, middle)
    thin = (chip == 2) if square else (col < 0)

    load = pltpu.make_async_copy(a_hbm, work, lsem.at[0])
    load_pivots = pltpu.make_async_copy(piv_any, piv_ref, lsem.at[1])
    load_seed = pltpu.make_async_copy(seed_any.at[0], approx, lsem.at[2])
    for copy in (load, load_pivots, load_seed):
        copy.start()
    barrier = pltpu.get_barrier_semaphore()
    for step in range(1, nrow):
        pl.semaphore_signal(
            barrier, inc=1, device_id=(col, lax.rem(row + step, nrow)), device_id_type=MESH
        )
    for step in range(1, ncol):
        pl.semaphore_signal(
            barrier, inc=1, device_id=(lax.rem(col + step, ncol), row), device_id_type=MESH
        )
    pl.semaphore_wait(barrier, nrow + ncol - 2)
    load.wait()

    def row_out(r):
        return pltpu.make_async_copy(work.at[r], out_any.at[r], osem.at[r])

    @pl.loop(0, first)
    def _(r):
        row_out(r).start()

    @pl.loop(col + HB + 1, work.shape[0])
    def _(r):
        row_out(r).start()


    def start(copy):
        copy.start()

    def share_copy(k, slot, source, target):
        return pltpu.make_async_remote_copy(
            src_ref=upper.at[k, source],
            dst_ref=upper.at[k, source],
            send_sem=usend.at[k, slot],
            recv_sem=urecv.at[k, source],
            device_id=(col, target),
            device_id_type=MESH,
        )

    end = (row == 0) | (row == 3)
    ahead = jnp.where(row < 2, 1, -1)

    def own_sends(k, act):
        if not square:
            for step in range(1, nrow):
                act(share_copy(k, step, row, lax.rem(row + step, nrow)))
            return
        act(share_copy(k, 1, row, row + ahead))

        @pl.when(~end)
        def _():
            act(share_copy(k, 2, row, row - ahead))

    def second_sends(k, act, far=True):
        if not square:
            return

        @pl.when(end)
        def _():
            if far:
                act(share_copy(k, 2, row, row + 3 * ahead))
            act(share_copy(k, 3, row, row + 2 * ahead))

        @pl.when(~end)
        def _():
            act(share_copy(k, 3, row + ahead, row - ahead))

    def start_gather(k):
        upper[k, row] = work[k]
        own_sends(k, start)

    def wait_share(k, source):
        share_copy(k, 0, source, source).wait_recv()

    def relay(k):
        if square:
            wait_share(k, row + ahead)
            @pl.when((core == 1) & (k < col))
            def _():
                pl.semaphore_wait(turn_sem, 1)

            second_sends(k, start)

    def pass_turn(k):
        if square:
            @pl.when(core == 0)
            def _():
                @pl.when(end)
                def _():
                    share_copy(k, 2, row, row + 3 * ahead).wait_send()

                pl.semaphore_signal(turn_sem, inc=1, device_id=(col + 1, row), device_id_type=MESH)

    def sources():
        if not square:
            return [lax.rem(row + step, nrow) for step in range(1, nrow)]
        return [jnp.where(end, row + 3 * ahead, row - ahead), row + 2 * ahead]

    def finish_gather(k):
        for source in sources():
            wait_share(k, source)

    def mult_copy(k, c, slot, target):
        return pltpu.make_async_remote_copy(
            src_ref=mult.at[k, c],
            dst_ref=mult.at[k, c],
            send_sem=msend.at[k, c, slot],
            recv_sem=mrecv.at[k, c],
            device_id=(target, row),
            device_id_type=MESH,
        )

    def forward(k, c, act, near=True, x=True, y=True):
        if not square:
            @pl.when((col + 1 < ncol) & (col + 1 <= k + HB))
            def _():
                act(mult_copy(k, c, 0, col + 1))

            return
        mine = k == col
        leads = ~mine & (core == 0)
        first_part = (k == 0) & (c < middle)
        along_y = (mine & (chip < 2)) | (leads & first_part & (chip == 1))
        along_x = (mine & ((chip == 0) | (chip == 2))) | (leads & (k < 2) & ~first_part & (chip == 2))
        across = mine & (chip == 1)

        if near:
            @pl.when(core == 0)
            def _():
                act(mult_copy(k, c, 0, col + 1))

        if x is not False:
            @pl.when((along_x | across) & x)
            def _():
                other = jnp.where(across, 2, chip + 1 - 2 * lax.rem(chip, 2))
                act(mult_copy(k, c, 1, 2 * other))

        if y is not False:
            @pl.when(along_y & y)
            def _():
                act(mult_copy(k, c, 2, 2 * (chip + 2)))

    def one_hot(k):
        ordering = jnp.broadcast_to(piv_ref[pl.ds(k, 1), :], (width, width))
        hits = lax.broadcasted_iota(jnp.int32, (width, width), 0) == ordering
        return jnp.where(hits, 1.0, 0.0).astype(BF16)

    def store_swapped(k):
        ordering = piv_ref[pl.ds(k, 1), :]
        mine = ordering[:, :share]
        for other in range(1, nrow):
            mine = jnp.where(row == other, ordering[:, other * share:(other + 1) * share], mine)
        hits = lax.broadcasted_iota(jnp.int32, (width, share), 0) == jnp.broadcast_to(mine, (width, share))
        hits = jnp.where(hits, 1.0, 0.0).astype(BF16)
        parts = split3(upper[k].reshape(width, width))
        contract = (((0,), (0,)), ((), ()))
        pick = lambda part: lax.dot_general(hits, part, contract, preferred_element_type=F32)
        work[k] = pick(parts[0]) + (pick(parts[1]) + pick(parts[2]))
        row_out(k).start()

    def split_upper(k):
        high, low = split(upper[k].reshape(width, width))
        u_high[k] = high
        u_low[k] = low

    def chunk(k, c):
        mult_copy(k, c, 0, col).wait_recv()
        forward(k, c, start)
        change = dot3(split(mult[k, c]), (u_high[k], u_low[k]))
        work[k + 1 + c] = work[k + 1 + c] - change

    def drain(k, carry):
        own_sends(k, lambda copy: copy.wait_send())

        second_sends(k, lambda copy: copy.wait_send(), far=False)

        @pl.when(early & end)
        def _():
            share_copy(k, 2, row, row + 3 * ahead).wait_send()

        @pl.loop(0, HB)
        def _(c):
            @pl.when(k < ncol - 1)
            def _():
                forward(k, c, lambda copy: copy.wait_send())

        return carry

    start_gather(first)

    load_pivots.wait()
    scatter = one_hot(col)
    order[...] = scatter
    load_seed.wait()
    seed_parts = split3(approx[...])
    contract = (((1,), (1,)), ((), ()))
    total = lax.dot_general(seed_parts[2], scatter, contract, preferred_element_type=F32)
    total += lax.dot_general(seed_parts[1], scatter, contract, preferred_element_type=F32)
    total += lax.dot_general(seed_parts[0], scatter, contract, preferred_element_type=F32)
    approx[...] = total
    high, low = split(total)
    x_high[...] = high
    x_low[...] = low
    relay(first)

    @pl.when(first < col)
    def _():
        pass_turn(first)

    def rest(k, skip=0):
        @pl.when(k >= first)
        def _():
            @pl.loop(jnp.where(thin & (k == 2), 3 + skip, middle), HB)
            def _(c):
                chunk(k, c)

    def update(k, carry):
        finish_gather(k)
        split_upper(k)
        chunk(k, 0)

        start_gather(k + 1)
        relay(k + 1)
        chunk(k, 1)

        @pl.when(thin & (k == 3))
        def _():
            chunk(k - 1, 2)

        @pl.when(k + 1 < col)
        def _():
            pass_turn(k + 1)

        @pl.when(k + 1 < busy)
        def _():
            rest(k - 1)

            @pl.loop(2, jnp.where(thin & (k == 2), 2, middle))
            def _(c):
                chunk(k, c)

        store_swapped(k)
        return carry

    lax.fori_loop(first, col, update, 0)

    def overdue(skip):
        rest(col - 3, skip)

        @pl.when(col - 2 >= first)
        def _():
            @pl.loop(2 + skip, HB)
            def _(c):
                chunk(col - 2, c)

        @pl.when(col > first)
        def _():
            @pl.loop(2, HB)
            def _(c):
                chunk(col - 1, c)

    @pl.when(early & ~final & (col - 2 >= first))
    def _():
        chunk(col - 2, 2)

        @pl.when(thin & (col == 5))
        def _():
            chunk(col - 3, 3)

    @pl.when(final)
    def _():
        overdue(0)
        lax.fori_loop(first, col - 1, drain, 0)

    seed = (x_high[...], x_low[...])
    mult[col, 0] = dot3(split(work[col + 1]), seed)

    def residual(source):
        high, low = split(upper[col, source])
        rows = lax.broadcasted_iota(jnp.int32, (share, width), 0) + source * share
        unit = jnp.where(rows == lax.broadcasted_iota(jnp.int32, (share, width), 1), 1.0, 0.0)
        left = unit - dot3((high, low), (x_high[...], x_low[...]))
        high, low = split(left)
        e_high[source] = high
        e_low[source] = low

    residual(row)
    if square:
        residual(row + ahead)
    pass_turn(col)
    for source in sources():
        wait_share(col, source)
        residual(source)
    error = (e_high[...].reshape(width, width), e_low[...].reshape(width, width))

    @pl.when(col < ncol - 1)
    def _():
        product = mult[col, 0]
        product = product + dot3(split(product), error)
        mult[col, 0] = product + dot3(split(dot3(split(product), error)), error)
        forward(col, 0, start)

    if square:
        @pl.when(core == 1)
        def _():
            pl.semaphore_signal(go_sem, inc=1, device_id=(col - 1, row), device_id_type=MESH)

    error = (e_high[...].reshape(width, width), e_low[...].reshape(width, width))
    better = approx[...] + dot3((x_high[...], x_low[...]), error)
    better = better + dot3(split(better), split(dot3(error, error)))

    high, low = split(better)

    @pl.when(col == ncol - 1)
    def _():
        target = order[...]
        x_high[...] = dot(high, target).astype(BF16)
        x_low[...] = dot(low, target).astype(BF16)

    @pl.when(col < ncol - 1)
    def _():
        x_high[...] = high
        x_low[...] = low

    @pl.when(~early)
    def _():
        rest(col - 2)

    @pl.when(early & ~final)
    def _():
        overdue(1)

    @pl.loop(jnp.where(col < ncol - 1, 1, 0), HB)
    def _(c):
        @pl.when((col > first) & ~early & (c > 0) & (c + 1 < HB))
        def _():
            chunk(col - 1, c + 1)

        last = dot3(split(work[col + 1 + c]), (x_high[...], x_low[...]))

        @pl.when(col < ncol - 1)
        def _():
            mult[col, c] = last
            forward(col, c, start, x=~holds | (c < sent_x), y=~holds | (c < middle))

        @pl.when(col == ncol - 1)
        def _():
            work[col + 1 + c] = last
            row_out(col + 1 + c).start()

    store_swapped(col)

    def permute(c):
        parts = split3(mult[col, c])
        target = order[...]
        work[col + 1 + c] = dot(parts[0], target) + (dot(parts[1], target) + dot(parts[2], target))
        row_out(col + 1 + c).start()

    @pl.when(col < ncol - 1)
    def _():
        @pl.loop(0, HB)
        def _(c):
            permute(c)

    if square:
        @pl.when(core == 0)
        def _():
            pl.semaphore_wait(go_sem, 1)

            @pl.loop(2, HB)
            def _(c):
                forward(col, c, start, near=False, x=c >= sent_x, y=c >= middle)

    lax.fori_loop(jnp.where(final, jnp.maximum(first, col - 1), first), col + 1, drain, 0)

    @pl.loop(0, work.shape[0])
    def _(r):
        row_out(r).wait()


def local(matrix, pivots, seeds):
    ncol = lax.axis_size("col")
    nrow = lax.axis_size("row")
    nblk, share, width = matrix.shape
    anywhere = pl.BlockSpec(memory_space=pl.ANY)
    half = pltpu.VMEM((width, width), BF16)
    words = 2 * nblk * share * width + ncol * width * width * 2 + ncol * HB * share * width + 6 * width * width
    limit = min(4 * words + 2**20, 60 * 1024 * 1024)
    return pl.pallas_call(
        functools.partial(kernel, ncol, nrow),
        out_shape=jax.ShapeDtypeStruct(matrix.shape, F32),
        in_specs=[anywhere] * 3,
        out_specs=anywhere,
        scratch_shapes=[
            pltpu.VMEM(pivots.shape, jnp.int32),
            pltpu.VMEM(matrix.shape, F32),
            pltpu.VMEM((ncol, nrow, share, width), F32),
            pltpu.VMEM((ncol, HB, share, width), F32),
            pltpu.VMEM((ncol, width, width), BF16),
            pltpu.VMEM((ncol, width, width), BF16),
            pltpu.VMEM((width, width), F32),
            half,
            half,
            pltpu.VMEM((nrow, share, width), BF16),
            pltpu.VMEM((nrow, share, width), BF16),
            half,
            pltpu.SemaphoreType.DMA((ncol, nrow)),
            pltpu.SemaphoreType.DMA((ncol, nrow)),
            pltpu.SemaphoreType.DMA((ncol, HB, 3)),
            pltpu.SemaphoreType.DMA((ncol, HB)),
            pltpu.SemaphoreType.DMA((3,)),
            pltpu.SemaphoreType.REGULAR,
            pltpu.SemaphoreType.REGULAR,
            pltpu.SemaphoreType.DMA((nblk,)),
        ],
        compiler_params=pltpu.CompilerParams(
            collective_id=0, has_side_effects=True, vmem_limit_bytes=limit
        ),
    )(matrix, pivots, seeds)


def solution(mesh):
    return jax.shard_map(
        local,
        mesh=mesh,
        in_specs=(P(None, "row", "col"), P(), P("col", None, None)),
        out_specs=P(None, "row", "col"),
        check_vma=False,
    )
```
